128 devices in a mesh: site: 8 (over z, core), col: 16 (over x, y).
Axes of the slice: x: 4, y: 4, z: 4, core: 2. Of those that a mesh axis runs over, the one named last changes fastest.
Arguments:
- common_geno: bfloat16 [8192, 32768], P(('site', 'col')), may hold values from 0 to 2
- rare_values: bfloat16 [2048, 512, 256], P(('site', 'col')), may hold values from -24 to 24
- block_tile: int32 [2048], P(('site', 'col')), may hold values from 0 to 127, as said below
- panel_rare: bfloat16 [65536, 512], P(('site', 'col')), may hold values from -24 to 24
Outputs:
- grm_panel: float32 [512, 32768], P(None, ('site', 'col'))
The draws below stay inside these ranges and needn't reach their ends.
Inputs may be any that keep to these rules, and one draw needn't show every extreme that they name: `block_tile`: the 16 listed blocks of device d in the site+col order (entries d * 16 to (d + 1) * 16 - 1) lie in distinct tiles; at most 2 of them lie in tiles t with one value of (t) mod 16.
All inputs are finite; a program needn't handle non-finite values.
Results may differ from the reference program's by a relative error of at most 0.0003.
Values may be sent and summed in bfloat16 or wider, within the bound.
No kernel may reach another device: no remote copies, remote signals or barrier semaphores. Data moves between devices by JAX's collectives and lax.ppermute only.
A program may use at most 192 MiB of HBM per device.

```python
import jax
import jax.numpy as jnp
from jax import lax

TILE = 256
PANEL = 512
SBLK = 512
CS_DEV = 64
TILES_DEV = 1
BLK_DEV = 16
S = 32768
M_C = 8192
RSITES = 65536
NBLK = 2048
NTILES = 128
N_SITE = 8
N_COL = 16


def draw_common_geno(key, part):
    key_pop = jax.random.fold_in(key, 11)
    key_freq = jax.random.fold_in(key, 12)
    key_unit = jax.random.fold_in(key, 13)
    population = jax.random.randint(key_pop, (S,), 0, 4)
    frequency = jax.random.uniform(key_freq, (4, M_C), jnp.float32, 0.05, 0.5)
    unit_draw = jax.random.uniform(key_unit, (M_C, S), jnp.float32)
    per_sample = jnp.take(frequency.T, population, axis=1)
    return (4.0 * per_sample * unit_draw).astype(jnp.bfloat16)


def draw_block_tile(key, part):
    device_count = N_SITE * N_COL
    per_col = TILES_DEV * N_SITE
    key_weight = jax.random.fold_in(key, 21)
    key_hot = jax.random.fold_in(key, 22)
    key_colnoise = jax.random.fold_in(key, 23)
    key_tileweight = jax.random.fold_in(key, 24)
    key_tilenoise = jax.random.fold_in(key, 25)
    col_ids = jnp.arange(N_COL, dtype=jnp.int32)
    col_weight = jax.random.randint(key_weight, (N_COL,), 0, 8)
    hot_col = jax.random.randint(key_hot, (), 0, N_COL)
    col_weight = jnp.where(col_ids == hot_col, 100, col_weight)
    col_score = (col_weight[None, :] * 64 + jax.random.randint(key_colnoise, (device_count, N_COL), 0, 64)) * N_COL + col_ids[None, :]
    col_order = jnp.argsort(-col_score, axis=1, stable=True)
    col_rank = jnp.argsort(col_order, axis=1, stable=True)
    counts = jnp.where(col_rank < N_COL // 4, 2, jnp.where(col_rank < 3 * N_COL // 4, 1, 0))
    place_ids = jnp.arange(per_col, dtype=jnp.int32)
    tile_weight = jax.random.randint(key_tileweight, (N_COL, per_col), 0, 4)
    tile_score = (tile_weight[None] * 64 + jax.random.randint(key_tilenoise, (device_count, N_COL, per_col), 0, 64)) * per_col + place_ids
    tile_order = jnp.argsort(-tile_score, axis=2, stable=True)[:, :, :2]
    owner_site = tile_order // TILES_DEV
    within = tile_order % TILES_DEV
    tile_ids = (owner_site * N_COL + col_ids[None, :, None]) * TILES_DEV + within
    valid = jnp.arange(2, dtype=jnp.int32)[None, None, :] < counts[:, :, None]
    flat_tiles = tile_ids.reshape(device_count, 2 * N_COL)
    flat_valid = valid.reshape(device_count, 2 * N_COL)
    keep_order = jnp.argsort(1 - flat_valid.astype(jnp.int32), axis=1, stable=True)[:, :N_COL]
    chosen = jnp.take_along_axis(flat_tiles, keep_order, axis=1)
    return chosen.reshape(device_count * N_COL).astype(jnp.int32)


def shard_levels(stream_key, dims, split, low, high):
    loudness = 1.0
    for axis_at, parts in split:
        draws = jax.random.uniform(jax.random.fold_in(jax.random.fold_in(stream_key, 6), axis_at), (parts,), jnp.float32, low / len(split), high / len(split))
        loudness = loudness * jnp.repeat(jnp.exp(draws), dims[axis_at] // parts).reshape((-1,) + (1,) * (len(dims) - 1 - axis_at))
    return loudness


def centred(own_key, dims, deviation, bound, pieces=(), kind=jnp.bfloat16):
    result = deviation * jax.random.normal(own_key, dims, jnp.float32)
    if pieces:
        result = result * shard_levels(own_key, dims, pieces, -0.22, 0.18)
    return jnp.clip(result, -bound, bound).astype(kind)


def setup_inputs(seed: int = 0) -> dict:
    keys = jax.random.split(jax.random.key(seed), 5)
    return {
        "common_geno": draw_common_geno(jax.random.fold_in(keys[4], 71), 0),
        "rare_values": centred(keys[1], (NBLK, SBLK, TILE), 4.0, 24.0, ((0, 128),)),
        "block_tile": draw_block_tile(jax.random.fold_in(keys[4], 71), 0),
        "panel_rare": centred(keys[3], (RSITES, PANEL), 4.0, 24.0, ((0, 128),)),
    }


epsilon = 1e-05

def standardize(block, sample_count):
    values = block.astype(jnp.float32)
    allele_freq = lax.optimization_barrier(jnp.sum(values, axis=1, keepdims=True)) / (2.0 * sample_count)
    scaling = lax.rsqrt(2.0 * allele_freq * (1.0 - allele_freq) + epsilon)
    return ((values - 2.0 * allele_freq) * scaling).astype(jnp.bfloat16)

def reference(common_geno, rare_values, block_tile, panel_rare):

    def common_step(index, summed):
        block = lax.dynamic_slice_in_dim(common_geno, index * CS_DEV, CS_DEV, 0)
        scaled = standardize(block, S).astype(jnp.float32)
        return summed + lax.dot_general(scaled[:, :PANEL], scaled, (((0,), (0,)), ((), ())), precision=lax.Precision.HIGHEST, preferred_element_type=jnp.float32)
    common = lax.fori_loop(0, M_C // CS_DEV, common_step, jnp.zeros((PANEL, S), jnp.float32))

    def rare_step(index, placed):
        values = lax.dynamic_slice_in_dim(rare_values, index * BLK_DEV, BLK_DEV, 0).astype(jnp.float32)
        panel_part = lax.dynamic_slice_in_dim(panel_rare, index * SBLK, SBLK, 0).astype(jnp.float32)
        tiles_here = lax.dynamic_slice_in_dim(block_tile, index * BLK_DEV, BLK_DEV, 0)
        products = jnp.einsum('si,ksj->ikj', panel_part, values, precision=lax.Precision.HIGHEST)
        return placed.at[:, tiles_here, :].add(products)
    placed = lax.fori_loop(0, NBLK // BLK_DEV, rare_step, jnp.zeros((PANEL, NTILES, TILE), jnp.float32))
    return (common + placed.reshape(PANEL, S)) / M_C
```

```python
import jax
import jax.numpy as jnp
from jax import lax
from jax.experimental import pallas as pl
from jax.experimental.pallas import tpu as pltpu
from jax.sharding import PartitionSpec as P


epsilon = 1e-05
BF = jnp.bfloat16
F32 = jnp.float32
NX = 4
NY = 4
NZ = 4
N_SITE = 8
N_COL = 16
TILE = 256
PANEL = 512
SBLK = 512
BLKS = 16
SLICE = TILE // N_SITE
VLIM = 60 * 1024 * 1024


def spec(shape, index_map):
    return pl.BlockSpec(shape, index_map)


def whole_vmem():
    return pl.BlockSpec(memory_space=pltpu.VMEM)


def pack_body(off_ref, x_ref, *rest):
    outs, turned = rest[:N_SITE], rest[N_SITE]
    for b in range(x_ref.shape[0]):
        turned[...] = x_ref[b].T
        for q in range(N_SITE):
            start = pl.multiple_of(off_ref[q], SLICE)
            outs[q][b * SLICE : (b + 1) * SLICE, :] = turned[pl.ds(start, SLICE), :]


def pack(rare_values, offsets):
    per = 2
    return pl.pallas_call(
        pack_body,
        grid_spec=pltpu.PrefetchScalarGridSpec(
            num_scalar_prefetch=1,
            grid=(BLKS // per,),
            in_specs=[spec((per, SBLK, TILE), lambda k, off: (k, 0, 0))],
            out_specs=[spec((per * SLICE, SBLK), lambda k, off: (k, 0))] * N_SITE,
            scratch_shapes=[pltpu.VMEM((TILE, SBLK), BF)],
        ),
        out_shape=[jax.ShapeDtypeStruct((BLKS * SLICE, SBLK), BF)] * N_SITE,
        compiler_params=pltpu.CompilerParams(vmem_limit_bytes=VLIM),
        cost_estimate=pl.CostEstimate(flops=0, bytes_accessed=8 << 20, transcendentals=0),
        name="pack_rare",
    )(offsets, rare_values)


def scale_body(x_ref, out_ref):
    rows, samples = x_ref.shape
    tiles = samples // TILE
    total = jnp.zeros((rows, TILE), F32)
    for t in range(tiles):
        total = total + x_ref[:, t * TILE : (t + 1) * TILE].astype(F32)
    freq = jnp.sum(total, axis=1, keepdims=True) / (2.0 * samples)
    scaling = lax.rsqrt(2.0 * freq * (1.0 - freq) + epsilon)
    mean = 2.0 * freq
    width = tiles // N_COL * TILE
    for t in range(tiles):
        scaled = ((x_ref[:, t * TILE : (t + 1) * TILE].astype(F32) - mean) * scaling).astype(BF)
        at = t // N_COL * TILE
        out_ref[t % N_COL, :, at : at + TILE] = scaled
        if t < PANEL // TILE:
            for c in range(N_COL):
                out_ref[c, :, width + t * TILE : width + (t + 1) * TILE] = scaled


def scale(common_geno):
    sites, samples = common_geno.shape
    rows = 16
    width = samples // N_COL + PANEL
    return pl.pallas_call(
        scale_body,
        grid=(sites // rows,),
        in_specs=[spec((rows, samples), lambda i: (i, 0))],
        out_specs=spec((N_COL, rows, width), lambda i: (0, i, 0)),
        out_shape=jax.ShapeDtypeStruct((N_COL, sites, width), BF),
        compiler_params=pltpu.CompilerParams(vmem_limit_bytes=VLIM),
        cost_estimate=pl.CostEstimate(flops=0, bytes_accessed=9 << 20, transcendentals=0),
        name="scale_common",
    )(common_geno)


def common_body(dest_ref, panel_ref, owned_ref, *rest):
    outs, turned = rest[:N_SITE], rest[N_SITE]
    step = pl.program_id(0)

    @pl.when(step == 0)
    def _():
        turned[...] = panel_ref[...].T

    part = jnp.dot(turned[...], owned_ref[...], preferred_element_type=F32)
    for q in range(N_SITE):

        @pl.when(step == q)
        def _():
            outs[q][...] = part


def common_product(received, dests):
    sites = received.shape[0] * received.shape[1]
    flat = received.reshape(sites, received.shape[2])
    last = (received.shape[2] - PANEL) // PANEL
    return pl.pallas_call(
        common_body,
        grid_spec=pltpu.PrefetchScalarGridSpec(
            num_scalar_prefetch=1,
            grid=(N_SITE,),
            in_specs=[
                spec((sites, PANEL), lambda q, dest: (0, last)),
                spec((sites, TILE), lambda q, dest: (0, dest[q])),
            ],
            out_specs=[spec((PANEL, TILE), lambda q, dest: (0, 0))] * N_SITE,
            scratch_shapes=[pltpu.VMEM((PANEL, sites), BF)],
        ),
        out_shape=[jax.ShapeDtypeStruct((PANEL, TILE), F32)] * N_SITE,
        compiler_params=pltpu.CompilerParams(vmem_limit_bytes=VLIM),
        cost_estimate=pl.CostEstimate(
            flops=2 * sites * PANEL * TILE * N_SITE, bytes_accessed=9 << 20, transcendentals=0
        ),
        name="common_product",
    )(dests, flat, flat)


HALF = 64


def rare_body(place_ref, *refs):
    slices = refs[:N_SITE]
    panels = refs[N_SITE : 2 * N_SITE]
    outs = refs[2 * N_SITE : 2 * N_SITE + 10]
    acc, made, sem = refs[2 * N_SITE + 10 :]
    acc[...] = jnp.zeros_like(acc)
    for q in range(N_SITE):
        made[...] = jnp.dot(
            slices[q][...], panels[q][:SBLK, :], preferred_element_type=F32
        )
        for k in range(BLKS):
            at = place_ref[q * BLKS + k]
            acc[at] = acc[at] + made[k * SLICE : (k + 1) * SLICE, :]
    copies = []
    for h in range(2):
        base = h * HALF
        up, down, keep1, keep3, own = outs[5 * h : 5 * h + 5]

        def unit(u, lo, hi):
            return acc.at[base + u * 16 + lo : base + u * 16 + hi]

        copies += [
            (unit(2, 0, 8), up.at[0:8]),
            (unit(1, 8, 16), up.at[8:16]),
            (unit(2, 8, 16), down.at[0:8]),
            (unit(3, 0, 8), down.at[8:16]),
            (unit(1, 0, 8), keep1),
            (unit(3, 8, 16), keep3),
            (unit(0, 0, 16), own),
        ]
    started = [
        pltpu.make_async_copy(src, dst, sem.at[i]) for i, (src, dst) in enumerate(copies)
    ]
    for one in started:
        one.start()
    for one in started:
        one.wait()


def rare_product(places, slices, panels):
    half = [16, 16, 8, 8, 16]
    return pl.pallas_call(
        rare_body,
        in_specs=[pl.BlockSpec(memory_space=pltpu.SMEM)] + [whole_vmem()] * (2 * N_SITE),
        out_specs=[pl.BlockSpec(memory_space=pl.ANY)] * 10,
        out_shape=[jax.ShapeDtypeStruct((n, SLICE, PANEL), F32) for n in half + half],
        scratch_shapes=[
            pltpu.VMEM((2 * HALF, SLICE, PANEL), F32),
            pltpu.VMEM((BLKS * SLICE, PANEL), F32),
            pltpu.SemaphoreType.DMA((14,)),
        ],
        compiler_params=pltpu.CompilerParams(vmem_limit_bytes=VLIM),
        cost_estimate=pl.CostEstimate(
            flops=2 * N_SITE * BLKS * SLICE * SBLK * PANEL, bytes_accessed=16 << 20, transcendentals=0
        ),
        name="rare_product",
    )(places, *slices, *panels)


def finish_body(turned_ref, *refs):
    parts, out_ref = refs[:N_SITE], refs[N_SITE]
    total = parts[0][...]
    for part in parts[1:]:
        total = total + part[...]
    out_ref[...] = (total + turned_ref[...].T) * (1.0 / 8192)


def finish(turned, parts):
    rows = PANEL // 2
    return pl.pallas_call(
        finish_body,
        grid=(2,),
        in_specs=[spec((TILE, rows), lambda i: (0, i))]
        + [spec((rows, TILE), lambda i: (i, 0))] * N_SITE,
        out_specs=spec((rows, TILE), lambda i: (i, 0)),
        out_shape=jax.ShapeDtypeStruct((PANEL, TILE), F32),
        compiler_params=pltpu.CompilerParams(vmem_limit_bytes=VLIM),
        cost_estimate=pl.CostEstimate(flops=0, bytes_accessed=6 << 20, transcendentals=0),
        name="finish",
    )(turned, *parts)


def along_site(dz, flip):
    return [
        (z * 2 + core, (z + dz) % NZ * 2 + (core ^ flip)) for z in range(NZ) for core in range(2)
    ]


def along_x(step):
    return [(x * NY + y, (x + step) % NX * NY + y) for x in range(NX) for y in range(NY)]


def along_y(step):
    return [(x * NY + y, x * NY + (y + step) % NY) for x in range(NX) for y in range(NY)]


def ring(up, down, keep1, keep3, own, perm):
    n = keep1.shape[0]
    from_low = lax.ppermute(up, "col", perm(1))
    from_high = lax.ppermute(down, "col", perm(-1))
    low2 = lax.ppermute(keep1 + from_low[:n], "col", perm(1))
    high2 = lax.ppermute(keep3 + from_high[:n], "col", perm(-1))
    first = own[:n] + from_high[n:] + low2
    second = own[n:] + from_low[n:] + high2
    return first, second


def second_ring(first, second, perm):
    own, one = first[:4], first[4:]
    two, three = second[:4], second[4:]
    up = jnp.concatenate([two[:2], one[2:]], axis=0)
    down = jnp.concatenate([two[2:], three[:2]], axis=0)
    return ring(up, down, one[:2], three[2:], own, perm)


def per_device(common_geno, rare_values, block_tile, panel_rare):
    site = lax.axis_index("site")
    col = lax.axis_index("col")
    z, core = site // 2, site % 2
    x, y = col // NY, col % NY
    order = [(dz, flip) for dz in range(NZ) for flip in range(2)]
    dests = jnp.stack([(z + dz) % NZ * 2 + (core ^ flip) for dz, flip in order]).astype(jnp.int32)

    tile_row = jnp.zeros((16, PANEL), BF).at[0, :BLKS].set(block_tile.astype(BF))
    panel_plus = jnp.concatenate([panel_rare, tile_row], axis=0)
    near = [panel_plus] + [lax.ppermute(panel_plus, "site", along_site(dz, 0)) for dz in range(1, NZ)]
    far = [lax.ppermute(one, "site", along_site(0, 1)) for one in near]
    panels = [(near, far)[flip][dz] for dz, flip in order]

    scaled = scale(common_geno)
    received = lax.all_to_all(scaled, "col", split_axis=0, concat_axis=0, tiled=True)

    packed = pack(rare_values, dests * SLICE)
    slices = [packed[0]] + [
        lax.ppermute(packed[q], "site", along_site(*order[q])) for q in range(1, N_SITE)
    ]

    tiles = jnp.stack([one[SBLK, :BLKS] for one in panels]).astype(jnp.int32).reshape(-1)
    tile_site, tile_col = tiles // N_COL, tiles % N_COL
    u = (tile_col // NY - x) % NX
    v = (tile_col % NY - y) % NY
    places = jnp.where(tile_site < 4, u * 16 + v * 4, HALF + v * 16 + u * 4) + tile_site % 4
    ring_parts = rare_product(places.astype(jnp.int32), slices, panels)

    common = common_product(received, dests)
    common = [common[0]] + [
        lax.ppermute(common[q], "site", along_site(*order[q])) for q in range(1, N_SITE)
    ]

    a = ring(*ring_parts[:5], along_x)
    b = ring(*ring_parts[5:], along_y)
    a = second_ring(*a, along_y)
    b = second_ring(*b, along_x)
    reduced = jnp.concatenate([*a, *b], axis=0)
    turned = lax.all_to_all(reduced, "site", split_axis=0, concat_axis=0, tiled=True)
    return finish(turned.reshape(TILE, PANEL), common)


def solution(mesh):
    placed = (
        P(("site", "col"), None),
        P(("site", "col"), None, None),
        P(("site", "col")),
        P(("site", "col"), None),
    )
    return jax.shard_map(
        per_device, mesh=mesh, in_specs=placed, out_specs=P(None, ("site", "col")), check_vma=False
    )
```

```python
import jax
import jax.numpy as jnp
from jax import lax
from jax.experimental import pallas as pl
from jax.experimental.pallas import tpu as pltpu
from jax.sharding import PartitionSpec as P


epsilon = 1e-05
BF = jnp.bfloat16
F32 = jnp.float32
NX = 4
NY = 4
NZ = 4
N_SITE = 8
N_COL = 16
TILE = 256
PANEL = 512
SBLK = 512
BLKS = 16
SLICE = TILE // N_SITE
VLIM = 60 * 1024 * 1024


def spec(shape, index_map):
    return pl.BlockSpec(shape, index_map)


def whole_vmem():
    return pl.BlockSpec(memory_space=pltpu.VMEM)


def pack_body(off_ref, x_ref, *rest):
    outs, turned = rest[:N_SITE], rest[N_SITE]
    for b in range(x_ref.shape[0]):
        turned[...] = x_ref[b].T
        for q in range(N_SITE):
            start = pl.multiple_of(off_ref[q], SLICE)
            outs[q][b * SLICE : (b + 1) * SLICE, :] = turned[pl.ds(start, SLICE), :]


def pack(rare_values, offsets):
    per = 2
    return pl.pallas_call(
        pack_body,
        grid_spec=pltpu.PrefetchScalarGridSpec(
            num_scalar_prefetch=1,
            grid=(BLKS // per,),
            in_specs=[spec((per, SBLK, TILE), lambda k, off: (k, 0, 0))],
            out_specs=[spec((per * SLICE, SBLK), lambda k, off: (k, 0))] * N_SITE,
            scratch_shapes=[pltpu.VMEM((TILE, SBLK), BF)],
        ),
        out_shape=[jax.ShapeDtypeStruct((BLKS * SLICE, SBLK), BF)] * N_SITE,
        compiler_params=pltpu.CompilerParams(vmem_limit_bytes=VLIM),
        cost_estimate=pl.CostEstimate(flops=0, bytes_accessed=8 << 20, transcendentals=0),
        name="pack_rare",
    )(offsets, rare_values)


def scale_body(x_ref, out_ref):
    rows, samples = x_ref.shape
    tiles = samples // TILE
    total = jnp.zeros((rows, TILE), F32)
    for t in range(tiles):
        total = total + x_ref[:, t * TILE : (t + 1) * TILE].astype(F32)
    freq = jnp.sum(total, axis=1, keepdims=True) / (2.0 * samples)
    scaling = lax.rsqrt(2.0 * freq * (1.0 - freq) + epsilon)
    mean = 2.0 * freq
    width = tiles // N_COL * TILE
    for t in range(tiles):
        scaled = ((x_ref[:, t * TILE : (t + 1) * TILE].astype(F32) - mean) * scaling).astype(BF)
        at = t // N_COL * TILE
        out_ref[t % N_COL, :, at : at + TILE] = scaled
        if t < PANEL // TILE:
            for c in range(N_COL):
                out_ref[c, :, width + t * TILE : width + (t + 1) * TILE] = scaled


def scale(common_geno):
    sites, samples = common_geno.shape
    rows = 16
    width = samples // N_COL + PANEL
    return pl.pallas_call(
        scale_body,
        grid=(sites // rows,),
        in_specs=[spec((rows, samples), lambda i: (i, 0))],
        out_specs=spec((N_COL, rows, width), lambda i: (0, i, 0)),
        out_shape=jax.ShapeDtypeStruct((N_COL, sites, width), BF),
        compiler_params=pltpu.CompilerParams(vmem_limit_bytes=VLIM),
        cost_estimate=pl.CostEstimate(flops=0, bytes_accessed=9 << 20, transcendentals=0),
        name="scale_common",
    )(common_geno)


def common_body(dest_ref, panel_ref, owned_ref, *rest):
    outs, turned = rest[:N_SITE], rest[N_SITE]
    step = pl.program_id(0)

    @pl.when(step == 0)
    def _():
        turned[...] = panel_ref[...].T

    part = jnp.dot(turned[...], owned_ref[...], preferred_element_type=F32)
    for q in range(N_SITE):

        @pl.when(step == q)
        def _():
            outs[q][...] = part


def common_product(received, dests):
    sites = received.shape[0] * received.shape[1]
    flat = received.reshape(sites, received.shape[2])
    last = (received.shape[2] - PANEL) // PANEL
    return pl.pallas_call(
        common_body,
        grid_spec=pltpu.PrefetchScalarGridSpec(
            num_scalar_prefetch=1,
            grid=(N_SITE,),
            in_specs=[
                spec((sites, PANEL), lambda q, dest: (0, last)),
                spec((sites, TILE), lambda q, dest: (0, dest[q])),
            ],
            out_specs=[spec((PANEL, TILE), lambda q, dest: (0, 0))] * N_SITE,
            scratch_shapes=[pltpu.VMEM((PANEL, sites), BF)],
        ),
        out_shape=[jax.ShapeDtypeStruct((PANEL, TILE), F32)] * N_SITE,
        compiler_params=pltpu.CompilerParams(vmem_limit_bytes=VLIM),
        cost_estimate=pl.CostEstimate(
            flops=2 * sites * PANEL * TILE * N_SITE, bytes_accessed=9 << 20, transcendentals=0
        ),
        name="common_product",
    )(dests, flat, flat)


HALF = 64


def rare_body(place_ref, *refs):
    slices = refs[:N_SITE]
    panels = refs[N_SITE : 2 * N_SITE]
    outs = refs[2 * N_SITE : 2 * N_SITE + 10]
    acc, made, sem = refs[2 * N_SITE + 10 :]
    acc[...] = jnp.zeros_like(acc)
    for q in range(N_SITE):
        made[...] = jnp.dot(
            slices[q][...], panels[q][:SBLK, :], preferred_element_type=F32
        )
        for k in range(BLKS):
            at = place_ref[q * BLKS + k]
            acc[at] = acc[at] + made[k * SLICE : (k + 1) * SLICE, :]
    copies = []
    for h in range(2):
        base = h * HALF
        up, down, keep1, keep3, own = outs[5 * h : 5 * h + 5]

        def unit(u, lo, hi):
            return acc.at[base + u * 16 + lo : base + u * 16 + hi]

        copies += [
            (unit(2, 0, 8), up.at[0:8]),
            (unit(1, 8, 16), up.at[8:16]),
            (unit(2, 8, 16), down.at[0:8]),
            (unit(3, 0, 8), down.at[8:16]),
            (unit(1, 0, 8), keep1),
            (unit(3, 8, 16), keep3),
            (unit(0, 0, 16), own),
        ]
    started = [
        pltpu.make_async_copy(src, dst, sem.at[i]) for i, (src, dst) in enumerate(copies)
    ]
    for one in started:
        one.start()
    for one in started:
        one.wait()


def rare_product(places, slices, panels):
    half = [16, 16, 8, 8, 16]
    return pl.pallas_call(
        rare_body,
        in_specs=[pl.BlockSpec(memory_space=pltpu.SMEM)] + [whole_vmem()] * (2 * N_SITE),
        out_specs=[pl.BlockSpec(memory_space=pl.ANY)] * 10,
        out_shape=[jax.ShapeDtypeStruct((n, SLICE, PANEL), F32) for n in half + half],
        scratch_shapes=[
            pltpu.VMEM((2 * HALF, SLICE, PANEL), F32),
            pltpu.VMEM((BLKS * SLICE, PANEL), F32),
            pltpu.SemaphoreType.DMA((14,)),
        ],
        compiler_params=pltpu.CompilerParams(vmem_limit_bytes=VLIM),
        cost_estimate=pl.CostEstimate(
            flops=2 * N_SITE * BLKS * SLICE * SBLK * PANEL, bytes_accessed=16 << 20, transcendentals=0
        ),
        name="rare_product",
    )(places, *slices, *panels)


def finish_body(turned_ref, *refs):
    parts, out_ref = refs[:N_SITE], refs[N_SITE]
    total = parts[0][...]
    for part in parts[1:]:
        total = total + part[...]
    out_ref[...] = (total + turned_ref[...].T) * (1.0 / 8192)


def finish(turned, parts):
    rows = PANEL // 2
    return pl.pallas_call(
        finish_body,
        grid=(2,),
        in_specs=[spec((TILE, rows), lambda i: (0, i))]
        + [spec((rows, TILE), lambda i: (i, 0))] * N_SITE,
        out_specs=spec((rows, TILE), lambda i: (i, 0)),
        out_shape=jax.ShapeDtypeStruct((PANEL, TILE), F32),
        compiler_params=pltpu.CompilerParams(vmem_limit_bytes=VLIM),
        cost_estimate=pl.CostEstimate(flops=0, bytes_accessed=6 << 20, transcendentals=0),
        name="finish",
    )(turned, *parts)


def along_site(dz, flip):
    return [
        (z * 2 + core, (z + dz) % NZ * 2 + (core ^ flip)) for z in range(NZ) for core in range(2)
    ]


def along_x(step):
    return [(x * NY + y, (x + step) % NX * NY + y) for x in range(NX) for y in range(NY)]


def along_y(step):
    return [(x * NY + y, x * NY + (y + step) % NY) for x in range(NX) for y in range(NY)]


def ring_open(up, down, perm):
    return lax.ppermute(up, "col", perm(1)), lax.ppermute(down, "col", perm(-1))


def ring_close(arrived, keep1, keep3, own, perm):
    from_low, from_high = arrived
    n = keep1.shape[0]
    low2 = lax.ppermute(keep1 + from_low[:n], "col", perm(1))
    high2 = lax.ppermute(keep3 + from_high[:n], "col", perm(-1))
    first = own[:n] + from_high[n:] + low2
    second = own[n:] + from_low[n:] + high2
    return first, second


def ring(up, down, keep1, keep3, own, perm):
    return ring_close(ring_open(up, down, perm), keep1, keep3, own, perm)


def second_ring(first, second, perm):
    own, one = first[:4], first[4:]
    two, three = second[:4], second[4:]
    up = jnp.concatenate([two[:2], one[2:]], axis=0)
    down = jnp.concatenate([two[2:], three[:2]], axis=0)
    return ring(up, down, one[:2], three[2:], own, perm)


def per_device(common_geno, rare_values, block_tile, panel_rare):
    site = lax.axis_index("site")
    col = lax.axis_index("col")
    z, core = site // 2, site % 2
    x, y = col // NY, col % NY
    order = [(dz, flip) for dz in range(NZ) for flip in range(2)]
    dests = jnp.stack([(z + dz) % NZ * 2 + (core ^ flip) for dz, flip in order]).astype(jnp.int32)

    tile_row = jnp.zeros((16, PANEL), BF).at[0, :BLKS].set(block_tile.astype(BF))
    panel_plus = jnp.concatenate([panel_rare, tile_row], axis=0)
    near = [panel_plus] + [
        lax.ppermute(panel_plus, "site", along_site(dz, 0)) for dz in range(1, NZ)
    ]

    scaled = scale(common_geno)
    scaled, offsets = lax.optimization_barrier((scaled, dests * SLICE))
    received = lax.all_to_all(scaled, "col", split_axis=0, concat_axis=0, tiled=True)

    packed = pack(rare_values, offsets)
    far = [lax.ppermute(one, "site", along_site(0, 1)) for one in near]
    panels = [(near, far)[flip][dz] for dz, flip in order]
    slices = [packed[0]] + [
        lax.ppermute(packed[q], "site", along_site(*order[q])) for q in range(1, N_SITE)
    ]

    tiles = jnp.stack([one[SBLK, :BLKS] for one in panels]).astype(jnp.int32).reshape(-1)
    tile_site, tile_col = tiles // N_COL, tiles % N_COL
    u = (tile_col // NY - x) % NX
    v = (tile_col % NY - y) % NY
    places = jnp.where(tile_site < 4, u * 16 + v * 4, HALF + v * 16 + u * 4) + tile_site % 4
    ring_parts = rare_product(places.astype(jnp.int32), slices, panels)

    ring_parts, dests = lax.optimization_barrier((ring_parts, dests))
    common = common_product(received, dests)
    open_a = ring_open(*ring_parts[:2], along_x)
    open_b = ring_open(*ring_parts[5:7], along_y)
    common = [common[0]] + [
        lax.ppermute(common[q], "site", along_site(*order[q])) for q in range(1, N_SITE)
    ]

    a = ring_close(open_a, *ring_parts[2:5], along_x)
    b = ring_close(open_b, *ring_parts[7:], along_y)
    a = second_ring(*a, along_y)
    b = second_ring(*b, along_x)
    reduced = jnp.concatenate([*a, *b], axis=0)
    turned = lax.all_to_all(reduced, "site", split_axis=0, concat_axis=0, tiled=True)
    return finish(turned.reshape(TILE, PANEL), common)


def solution(mesh):
    placed = (
        P(("site", "col"), None),
        P(("site", "col"), None, None),
        P(("site", "col")),
        P(("site", "col"), None),
    )
    return jax.shard_map(
        per_device, mesh=mesh, in_specs=placed, out_specs=P(None, ("site", "col")), check_vma=False
    )
```

```python
import jax
import jax.numpy as jnp
from jax import lax
from jax.experimental import pallas as pl
from jax.experimental.pallas import tpu as pltpu
from jax.sharding import PartitionSpec as P


epsilon = 1e-05
BF = jnp.bfloat16
F32 = jnp.float32
NX = 4
NY = 4
NZ = 4
N_SITE = 8
N_COL = 16
TILE = 256
PANEL = 512
SBLK = 512
BLKS = 16
SLICE = TILE // N_SITE
VLIM = 60 * 1024 * 1024


def spec(shape, index_map):
    return pl.BlockSpec(shape, index_map)


def whole_vmem():
    return pl.BlockSpec(memory_space=pltpu.VMEM)


def pack_body(off_ref, x_ref, *rest):
    outs, turned = rest[:N_SITE], rest[N_SITE]
    for b in range(x_ref.shape[0]):
        turned[...] = x_ref[b].T
        for q in range(N_SITE):
            start = pl.multiple_of(off_ref[q], SLICE)
            outs[q][b * SLICE : (b + 1) * SLICE, :] = turned[pl.ds(start, SLICE), :]


def pack(rare_values, offsets):
    per = 2
    return pl.pallas_call(
        pack_body,
        grid_spec=pltpu.PrefetchScalarGridSpec(
            num_scalar_prefetch=1,
            grid=(BLKS // per,),
            in_specs=[spec((per, SBLK, TILE), lambda k, off: (k, 0, 0))],
            out_specs=[spec((per * SLICE, SBLK), lambda k, off: (k, 0))] * N_SITE,
            scratch_shapes=[pltpu.VMEM((TILE, SBLK), BF)],
        ),
        out_shape=[jax.ShapeDtypeStruct((BLKS * SLICE, SBLK), BF)] * N_SITE,
        compiler_params=pltpu.CompilerParams(vmem_limit_bytes=VLIM),
        cost_estimate=pl.CostEstimate(flops=0, bytes_accessed=8 << 20, transcendentals=0),
        name="pack_rare",
    )(offsets, rare_values)


def scale_body(x_ref, out_ref):
    rows, samples = x_ref.shape
    tiles = samples // TILE
    total = jnp.zeros((rows, TILE), F32)
    for t in range(tiles):
        total = total + x_ref[:, t * TILE : (t + 1) * TILE].astype(F32)
    freq = jnp.sum(total, axis=1, keepdims=True) / (2.0 * samples)
    scaling = lax.rsqrt(2.0 * freq * (1.0 - freq) + epsilon)
    mean = 2.0 * freq
    width = tiles // N_COL * TILE
    for t in range(tiles):
        scaled = ((x_ref[:, t * TILE : (t + 1) * TILE].astype(F32) - mean) * scaling).astype(BF)
        at = t // N_COL * TILE
        out_ref[t % N_COL, :, at : at + TILE] = scaled
        if t < PANEL // TILE:
            for c in range(N_COL):
                out_ref[c, :, width + t * TILE : width + (t + 1) * TILE] = scaled


def scale(common_geno):
    sites, samples = common_geno.shape
    rows = 16
    width = samples // N_COL + PANEL
    return pl.pallas_call(
        scale_body,
        grid=(sites // rows,),
        in_specs=[spec((rows, samples), lambda i: (i, 0))],
        out_specs=spec((N_COL, rows, width), lambda i: (0, i, 0)),
        out_shape=jax.ShapeDtypeStruct((N_COL, sites, width), BF),
        compiler_params=pltpu.CompilerParams(vmem_limit_bytes=VLIM),
        cost_estimate=pl.CostEstimate(flops=0, bytes_accessed=9 << 20, transcendentals=0),
        name="scale_common",
    )(common_geno)


def common_body(dest_ref, panel_ref, owned_ref, *rest):
    outs, turned = rest[:N_SITE], rest[N_SITE]
    step = pl.program_id(0)

    @pl.when(step == 0)
    def _():
        turned[...] = panel_ref[...].T

    part = jnp.dot(turned[...], owned_ref[...], preferred_element_type=F32)
    for q in range(N_SITE):

        @pl.when(step == q)
        def _():
            outs[q][...] = part


def common_product(received, dests):
    sites = received.shape[0] * received.shape[1]
    flat = received.reshape(sites, received.shape[2])
    last = (received.shape[2] - PANEL) // PANEL
    return pl.pallas_call(
        common_body,
        grid_spec=pltpu.PrefetchScalarGridSpec(
            num_scalar_prefetch=1,
            grid=(N_SITE,),
            in_specs=[
                spec((sites, PANEL), lambda q, dest: (0, last)),
                spec((sites, TILE), lambda q, dest: (0, dest[q])),
            ],
            out_specs=[spec((PANEL, TILE), lambda q, dest: (0, 0))] * N_SITE,
            scratch_shapes=[pltpu.VMEM((PANEL, sites), BF)],
        ),
        out_shape=[jax.ShapeDtypeStruct((PANEL, TILE), F32)] * N_SITE,
        compiler_params=pltpu.CompilerParams(vmem_limit_bytes=VLIM),
        cost_estimate=pl.CostEstimate(
            flops=2 * sites * PANEL * TILE * N_SITE, bytes_accessed=9 << 20, transcendentals=0
        ),
        name="common_product",
    )(dests, flat, flat)


HALF = 64


def rare_body(place_ref, *refs):
    slices = refs[:N_SITE]
    panels = refs[N_SITE : 2 * N_SITE]
    outs = refs[2 * N_SITE : 2 * N_SITE + 10]
    acc, made, sem = refs[2 * N_SITE + 10 :]
    acc[...] = jnp.zeros_like(acc)
    for q in range(N_SITE):
        made[...] = jnp.dot(
            slices[q][...], panels[q][:SBLK, :], preferred_element_type=F32
        )
        for k in range(BLKS):
            at = place_ref[q * BLKS + k]
            acc[at] = acc[at] + made[k * SLICE : (k + 1) * SLICE, :]
    copies = []
    for h in range(2):
        base = h * HALF
        up, down, keep1, keep3, own = outs[5 * h : 5 * h + 5]

        def unit(u, lo, hi):
            return acc.at[base + u * 16 + lo : base + u * 16 + hi]

        copies += [
            (unit(2, 0, 8), up.at[0:8]),
            (unit(1, 8, 16), up.at[8:16]),
            (unit(2, 8, 16), down.at[0:8]),
            (unit(3, 0, 8), down.at[8:16]),
            (unit(1, 0, 8), keep1),
            (unit(3, 8, 16), keep3),
            (unit(0, 0, 16), own),
        ]
    started = [
        pltpu.make_async_copy(src, dst, sem.at[i]) for i, (src, dst) in enumerate(copies)
    ]
    for one in started:
        one.start()
    for one in started:
        one.wait()


def rare_product(places, slices, panels):
    half = [16, 16, 8, 8, 16]
    return pl.pallas_call(
        rare_body,
        in_specs=[pl.BlockSpec(memory_space=pltpu.SMEM)] + [whole_vmem()] * (2 * N_SITE),
        out_specs=[pl.BlockSpec(memory_space=pl.ANY)] * 10,
        out_shape=[jax.ShapeDtypeStruct((n, SLICE, PANEL), F32) for n in half + half],
        scratch_shapes=[
            pltpu.VMEM((2 * HALF, SLICE, PANEL), F32),
            pltpu.VMEM((BLKS * SLICE, PANEL), F32),
            pltpu.SemaphoreType.DMA((14,)),
        ],
        compiler_params=pltpu.CompilerParams(vmem_limit_bytes=VLIM),
        cost_estimate=pl.CostEstimate(
            flops=2 * N_SITE * BLKS * SLICE * SBLK * PANEL, bytes_accessed=16 << 20, transcendentals=0
        ),
        name="rare_product",
    )(places, *slices, *panels)


def sum_body(*refs):
    total = refs[0][...]
    for part in refs[1:N_SITE]:
        total = total + part[...]
    refs[N_SITE][...] = total


def sum_parts(parts):
    rows = PANEL // 4
    return pl.pallas_call(
        sum_body,
        grid=(4,),
        in_specs=[spec((rows, TILE), lambda i: (i, 0))] * N_SITE,
        out_specs=spec((rows, TILE), lambda i: (i, 0)),
        out_shape=jax.ShapeDtypeStruct((PANEL, TILE), F32),
        compiler_params=pltpu.CompilerParams(vmem_limit_bytes=16 << 20),
        cost_estimate=pl.CostEstimate(flops=0, bytes_accessed=5 << 20, transcendentals=0),
        name="sum_parts",
    )(*parts)


def finish_body(turned_ref, common_ref, out_ref):
    out_ref[...] = (common_ref[...] + turned_ref[...].T) * (1.0 / 8192)


def finish(turned, common):
    rows = PANEL // 2
    return pl.pallas_call(
        finish_body,
        grid=(2,),
        in_specs=[
            spec((TILE, rows), lambda i: (0, i)),
            spec((rows, TILE), lambda i: (i, 0)),
        ],
        out_specs=spec((rows, TILE), lambda i: (i, 0)),
        out_shape=jax.ShapeDtypeStruct((PANEL, TILE), F32),
        compiler_params=pltpu.CompilerParams(vmem_limit_bytes=16 << 20),
        cost_estimate=pl.CostEstimate(flops=0, bytes_accessed=2 << 20, transcendentals=0),
        name="finish",
    )(turned, common)


def along_site(dz, flip):
    return [
        (z * 2 + core, (z + dz) % NZ * 2 + (core ^ flip)) for z in range(NZ) for core in range(2)
    ]


def along_x(step):
    return [(x * NY + y, (x + step) % NX * NY + y) for x in range(NX) for y in range(NY)]


def along_y(step):
    return [(x * NY + y, x * NY + (y + step) % NY) for x in range(NX) for y in range(NY)]


def ring_open(up, down, perm):
    return lax.ppermute(up, "col", perm(1)), lax.ppermute(down, "col", perm(-1))


def ring_close(arrived, keep1, keep3, own, perm):
    from_low, from_high = arrived
    n = keep1.shape[0]
    low2 = lax.ppermute(keep1 + from_low[:n], "col", perm(1))
    high2 = lax.ppermute(keep3 + from_high[:n], "col", perm(-1))
    first = own[:n] + from_high[n:] + low2
    second = own[n:] + from_low[n:] + high2
    return first, second


def direct(first, second, perm):
    far = lax.ppermute(second[:4], "col", perm(2))
    low = lax.ppermute(first[4:], "col", perm(1))
    high = lax.ppermute(second[4:], "col", perm(-1))
    return first[:4] + low + high + far


def per_device(common_geno, rare_values, block_tile, panel_rare):
    site = lax.axis_index("site")
    col = lax.axis_index("col")
    z, core = site // 2, site % 2
    x, y = col // NY, col % NY
    order = [(dz, flip) for dz in range(NZ) for flip in range(2)]
    dests = jnp.stack([(z + dz) % NZ * 2 + (core ^ flip) for dz, flip in order]).astype(jnp.int32)

    tile_row = jnp.zeros((16, PANEL), BF).at[0, :BLKS].set(block_tile.astype(BF))
    panel_plus = jnp.concatenate([panel_rare, tile_row], axis=0)
    near = [panel_plus] + [
        lax.ppermute(panel_plus, "site", along_site(dz, 0)) for dz in range(1, NZ)
    ]

    scaled = scale(common_geno)
    scaled, offsets = lax.optimization_barrier((scaled, dests * SLICE))
    received = lax.all_to_all(scaled, "col", split_axis=0, concat_axis=0, tiled=True)

    packed = pack(rare_values, offsets)
    far = [lax.ppermute(one, "site", along_site(0, 1)) for one in near]
    panels = [(near, far)[flip][dz] for dz, flip in order]
    slices = [packed[0]] + [
        lax.ppermute(packed[q], "site", along_site(*order[q])) for q in range(1, N_SITE)
    ]

    tiles = jnp.stack([one[SBLK, :BLKS] for one in panels]).astype(jnp.int32).reshape(-1)
    tile_site, tile_col = tiles // N_COL, tiles % N_COL
    u = (tile_col // NY - x) % NX
    v = (tile_col % NY - y) % NY
    places = jnp.where(tile_site < 4, u * 16 + v * 4, HALF + v * 16 + u * 4) + tile_site % 4
    ring_parts = rare_product(places.astype(jnp.int32), slices, panels)

    ring_parts, dests = lax.optimization_barrier((ring_parts, dests))
    common = common_product(received, dests)
    open_a = ring_open(*ring_parts[:2], along_x)
    open_b = ring_open(*ring_parts[5:7], along_y)
    common = [common[0]] + [
        lax.ppermute(common[q], "site", along_site(*order[q])) for q in range(1, N_SITE)
    ]

    a = ring_close(open_a, *ring_parts[2:5], along_x)
    b = ring_close(open_b, *ring_parts[7:], along_y)
    a = direct(*a, along_y)
    b = direct(*b, along_x)
    reduced = jnp.concatenate([*a, *b], axis=0)
    turned = lax.all_to_all(reduced, "site", split_axis=0, concat_axis=0, tiled=True)
    return finish(turned.reshape(TILE, PANEL), sum_parts(common))


def solution(mesh):
    placed = (
        P(("site", "col"), None),
        P(("site", "col"), None, None),
        P(("site", "col")),
        P(("site", "col"), None),
    )
    return jax.shard_map(
        per_device, mesh=mesh, in_specs=placed, out_specs=P(None, ("site", "col")), check_vma=False
    )
```

```python
import jax
import jax.numpy as jnp
from jax import lax
from jax.experimental import pallas as pl
from jax.experimental.pallas import tpu as pltpu
from jax.sharding import PartitionSpec as P


epsilon = 1e-05
BF = jnp.bfloat16
F32 = jnp.float32
NX = 4
NY = 4
NZ = 4
N_SITE = 8
N_COL = 16
TILE = 256
PANEL = 512
SBLK = 512
BLKS = 16
SLICE = TILE // N_SITE
VLIM = 24 * 1024 * 1024
WIDE = 60 * 1024 * 1024


def spec(shape, index_map):
    return pl.BlockSpec(shape, index_map)


def whole_vmem():
    return pl.BlockSpec(memory_space=pltpu.VMEM)


def pack_body(off_ref, x_ref, *rest):
    outs, turned = rest[:N_SITE], rest[N_SITE]
    for b in range(x_ref.shape[0]):
        turned[...] = x_ref[b].T
        for q in range(N_SITE):
            start = pl.multiple_of(off_ref[q], SLICE)
            outs[q][b * SLICE : (b + 1) * SLICE, :] = turned[pl.ds(start, SLICE), :]


def pack(rare_values, offsets):
    per = 2
    return pl.pallas_call(
        pack_body,
        grid_spec=pltpu.PrefetchScalarGridSpec(
            num_scalar_prefetch=1,
            grid=(BLKS // per,),
            in_specs=[spec((per, SBLK, TILE), lambda k, off: (k, 0, 0))],
            out_specs=[spec((per * SLICE, SBLK), lambda k, off: (k, 0))] * N_SITE,
            scratch_shapes=[pltpu.VMEM((TILE, SBLK), BF)],
        ),
        out_shape=[jax.ShapeDtypeStruct((BLKS * SLICE, SBLK), BF)] * N_SITE,
        compiler_params=pltpu.CompilerParams(vmem_limit_bytes=WIDE),
        cost_estimate=pl.CostEstimate(flops=0, bytes_accessed=8 << 20, transcendentals=0),
        name="pack_rare",
    )(offsets, rare_values)


def scale_body(x_ref, out_ref, panel_ref):
    rows, samples = x_ref.shape
    tiles = samples // TILE
    total = jnp.zeros((rows, TILE), F32)
    for t in range(tiles):
        total = total + x_ref[:, t * TILE : (t + 1) * TILE].astype(F32)
    freq = jnp.sum(total, axis=1, keepdims=True) / (2.0 * samples)
    scaling = lax.rsqrt(2.0 * freq * (1.0 - freq) + epsilon)
    mean = 2.0 * freq
    for t in range(tiles):
        scaled = ((x_ref[:, t * TILE : (t + 1) * TILE].astype(F32) - mean) * scaling).astype(BF)
        at = t // N_COL * TILE
        out_ref[t % N_COL, :, at : at + TILE] = scaled
        if t < PANEL // TILE:
            panel_ref[:, t * TILE : (t + 1) * TILE] = scaled


def scale(common_geno):
    sites, samples = common_geno.shape
    rows = 16
    width = samples // N_COL
    return pl.pallas_call(
        scale_body,
        grid=(sites // rows,),
        in_specs=[spec((rows, samples), lambda i: (i, 0))],
        out_specs=[
            spec((N_COL, rows, width), lambda i: (0, i, 0)),
            spec((rows, PANEL), lambda i: (i, 0)),
        ],
        out_shape=[
            jax.ShapeDtypeStruct((N_COL, sites, width), BF),
            jax.ShapeDtypeStruct((sites, PANEL), BF),
        ],
        compiler_params=pltpu.CompilerParams(vmem_limit_bytes=WIDE),
        cost_estimate=pl.CostEstimate(flops=0, bytes_accessed=9 << 20, transcendentals=0),
        name="scale_common",
    )(common_geno)


def common_body(dest_ref, row_ref, *refs):
    panels, owned_ref = refs[:NY], refs[NY]
    outs = refs[NY + 1 : NY + 2 + NZ]
    joined, turned = refs[NY + 2 + NZ :]
    step = pl.program_id(0)
    sites = joined.shape[0] // N_COL

    @pl.when(step == 0)
    def _():
        for dy in range(NY):
            for dx in range(NX):
                start = pl.multiple_of(row_ref[dy * NX + dx], sites)
                joined[pl.ds(start, sites), :] = panels[dy][dx * sites : (dx + 1) * sites, :]
        turned[...] = joined[...].T

    part = jnp.dot(turned[...], owned_ref[...], preferred_element_type=F32)
    for q in range(N_SITE):

        @pl.when(step == q)
        def _():
            if q < NZ:
                outs[NZ][q] = part
            else:
                outs[q - NZ][...] = part


def common_product(received, dests, rows, panels):
    sites = received.shape[0] * received.shape[1]
    flat = received.reshape(sites, received.shape[2])
    return pl.pallas_call(
        common_body,
        grid_spec=pltpu.PrefetchScalarGridSpec(
            num_scalar_prefetch=2,
            grid=(N_SITE,),
            in_specs=[spec(panels[0].shape, lambda q, dest, row: (0, 0))] * NY
            + [spec((sites, TILE), lambda q, dest, row: (0, dest[q]))],
            out_specs=[spec((PANEL, TILE), lambda q, dest, row: (0, 0))] * NZ
            + [spec((NZ, PANEL, TILE), lambda q, dest, row: (0, 0, 0))],
            scratch_shapes=[pltpu.VMEM((sites, PANEL), BF), pltpu.VMEM((PANEL, sites), BF)],
        ),
        out_shape=[jax.ShapeDtypeStruct((PANEL, TILE), F32)] * NZ
        + [jax.ShapeDtypeStruct((NZ, PANEL, TILE), F32)],
        compiler_params=pltpu.CompilerParams(vmem_limit_bytes=VLIM),
        cost_estimate=pl.CostEstimate(
            flops=2 * sites * PANEL * TILE * N_SITE, bytes_accessed=9 << 20, transcendentals=0
        ),
        name="common_product",
    )(dests, rows, *panels, flat)


HALF = 64
EARLY = 5


def accumulate(place_ref, slices, panels, acc, made, first):
    for q in range(len(slices)):
        made[...] = jnp.dot(slices[q][...], panels[q][:SBLK, :], preferred_element_type=F32)
        for k in range(BLKS):
            at = place_ref[(first + q) * BLKS + k]
            acc[at] = acc[at] + made[k * SLICE : (k + 1) * SLICE, :]


def early_body(place_ref, *refs):
    slices, panels = refs[:EARLY], refs[EARLY : 2 * EARLY]
    acc, made = refs[2 * EARLY :]
    acc[...] = jnp.zeros_like(acc)
    accumulate(place_ref, slices, panels, acc, made, 0)


def late_body(place_ref, acc_in, *refs):
    late = N_SITE - EARLY
    slices, panels = refs[:late], refs[late : 2 * late]
    acc = refs[2 * late]
    outs = refs[2 * late + 1 : 2 * late + 11]
    made, sem = refs[2 * late + 11 :]
    accumulate(place_ref, slices, panels, acc, made, EARLY)
    copies = []
    for h in range(2):
        base = h * HALF
        up, down, keep1, keep3, own = outs[5 * h : 5 * h + 5]

        def unit(u, lo, hi):
            return acc.at[base + u * 16 + lo : base + u * 16 + hi]

        copies += [
            (unit(2, 0, 8), up.at[0:8]),
            (unit(1, 8, 16), up.at[8:16]),
            (unit(2, 8, 16), down.at[0:8]),
            (unit(3, 0, 8), down.at[8:16]),
            (unit(1, 0, 8), keep1),
            (unit(3, 8, 16), keep3),
            (unit(0, 0, 16), own),
        ]
    started = [
        pltpu.make_async_copy(src, dst, sem.at[i]) for i, (src, dst) in enumerate(copies)
    ]
    for one in started:
        one.start()
    for one in started:
        one.wait()


def rare_cost(sources):
    return pl.CostEstimate(
        flops=2 * sources * BLKS * SLICE * SBLK * PANEL, bytes_accessed=sources << 20, transcendentals=0
    )


def rare_product(places, slices, panels):
    dense = (2 * HALF, SLICE, PANEL)
    smem = pl.BlockSpec(memory_space=pltpu.SMEM)
    acc = pl.pallas_call(
        early_body,
        in_specs=[smem] + [whole_vmem()] * (2 * EARLY),
        out_specs=whole_vmem(),
        out_shape=pltpu.VMEM(dense, F32),
        scratch_shapes=[pltpu.VMEM((BLKS * SLICE, PANEL), F32)],
        compiler_params=pltpu.CompilerParams(vmem_limit_bytes=24 << 20),
        cost_estimate=rare_cost(EARLY),
        name="rare_early",
    )(places, *slices[:EARLY], *panels[:EARLY])
    late = N_SITE - EARLY
    half = [pltpu.HBM((n, SLICE, PANEL), F32) for n in (16, 16, 8, 8, 16)]
    half_specs = [pl.BlockSpec(memory_space=pltpu.HBM)] * 5
    return pl.pallas_call(
        late_body,
        in_specs=[smem, whole_vmem()] + [whole_vmem()] * (2 * late),
        out_specs=[whole_vmem()] + half_specs * 2,
        out_shape=[pltpu.VMEM(dense, F32)] + half * 2,
        scratch_shapes=[
            pltpu.VMEM((BLKS * SLICE, PANEL), F32),
            pltpu.SemaphoreType.DMA((14,)),
        ],
        input_output_aliases={1: 0},
        compiler_params=pltpu.CompilerParams(vmem_limit_bytes=24 << 20),
        cost_estimate=rare_cost(late),
        name="rare_late",
    )(places, acc, *slices[EARLY:], *panels[EARLY:])[1:]


def sum_body(mine, swapped, a, b, c, out_ref):
    out_ref[...] = mine[...] + swapped[0] + a[...] + b[...] + c[...]


def sum_parts(parts):
    rows = PANEL // 4
    block = spec((rows, TILE), lambda i: (i, 0))
    return pl.pallas_call(
        sum_body,
        grid=(4,),
        in_specs=[block, spec((1, rows, TILE), lambda i: (0, i, 0)), block, block, block],
        out_specs=block,
        out_shape=jax.ShapeDtypeStruct((PANEL, TILE), F32),
        compiler_params=pltpu.CompilerParams(vmem_limit_bytes=16 << 20),
        cost_estimate=pl.CostEstimate(flops=0, bytes_accessed=3 << 20, transcendentals=0),
        name="sum_parts",
    )(*parts)


def finish_body(row_ref, common_ref, *refs):
    pieces, out_ref, turned = refs[:N_SITE], refs[N_SITE], refs[N_SITE + 1]
    for q in range(N_SITE):
        start = pl.multiple_of(row_ref[q], SLICE)
        turned[pl.ds(start, SLICE), :] = pieces[q][...]
    out_ref[...] = (common_ref[...] + turned[...].T) * (1.0 / 8192)


def finish(rows, common, pieces):
    return pl.pallas_call(
        finish_body,
        in_specs=[pl.BlockSpec(memory_space=pltpu.SMEM)] + [whole_vmem()] * (1 + N_SITE),
        out_specs=whole_vmem(),
        out_shape=jax.ShapeDtypeStruct((PANEL, TILE), F32),
        scratch_shapes=[pltpu.VMEM((TILE, PANEL), F32)],
        compiler_params=pltpu.CompilerParams(vmem_limit_bytes=16 << 20),
        cost_estimate=pl.CostEstimate(flops=0, bytes_accessed=2 << 20, transcendentals=0),
        name="finish",
    )(rows, common, *pieces)


def along_site(dz, flip):
    return [
        (z * 2 + core, (z + dz) % NZ * 2 + (core ^ flip)) for z in range(NZ) for core in range(2)
    ]


def along_x(step):
    return [(x * NY + y, (x + step) % NX * NY + y) for x in range(NX) for y in range(NY)]


def along_y(step):
    return [(x * NY + y, x * NY + (y + step) % NY) for x in range(NX) for y in range(NY)]


def ring_open(up, down, perm):
    return lax.ppermute(up, "col", perm(1)), lax.ppermute(down, "col", perm(-1))


PIECES = (8, SLICE, PANEL)


def piece(n, shift):
    return spec((n, SLICE, PANEL), lambda i: (i + shift, 0, 0))


def add_body(*refs):
    for h in range(4):
        refs[8 + h][...] = refs[2 * h][...] + refs[2 * h + 1][...]


def close_sums(open_a, open_b, keeps):
    args = []
    for arrived, keep in zip((*open_a, *open_b), keeps):
        args += [arrived, keep]
    return pl.pallas_call(
        add_body,
        grid=(2,),
        in_specs=[piece(4, 0)] * 8,
        out_specs=[piece(4, 0)] * 4,
        out_shape=[jax.ShapeDtypeStruct(PIECES, F32)] * 4,
        compiler_params=pltpu.CompilerParams(vmem_limit_bytes=VLIM),
        cost_estimate=pl.CostEstimate(flops=0, bytes_accessed=6 << 20, transcendentals=0),
        name="close_sums",
    )(*args)


def pre_sums(open_a, open_b, own_a, own_b):
    args, maps = [], []
    for (low, high), own in ((open_a, own_a), (open_b, own_b)):
        args += [own, high, own, low]
        maps += [piece(4, 0), piece(4, 2), piece(4, 2), piece(4, 2)]
    return pl.pallas_call(
        add_body,
        grid=(2,),
        in_specs=maps,
        out_specs=[piece(4, 0)] * 4,
        out_shape=[jax.ShapeDtypeStruct(PIECES, F32)] * 4,
        compiler_params=pltpu.CompilerParams(vmem_limit_bytes=VLIM),
        cost_estimate=pl.CostEstimate(flops=0, bytes_accessed=6 << 20, transcendentals=0),
        name="pre_sums",
    )(*args)


def line_body(*refs):
    step = pl.program_id(0)
    for h in range(4):
        total = refs[2 * h][...] + refs[2 * h + 1][...]
        for part in range(2):

            @pl.when(step == part)
            def _():
                refs[8 + 2 * h + part][...] = total


def line_sums(pre, closed):
    args = []
    for one, two in zip(pre, closed):
        args += [one, two]
    return pl.pallas_call(
        line_body,
        grid=(2,),
        in_specs=[piece(4, 0)] * 8,
        out_specs=[spec((4, SLICE, PANEL), lambda i: (0, 0, 0))] * 8,
        out_shape=[jax.ShapeDtypeStruct((4, SLICE, PANEL), F32)] * 8,
        compiler_params=pltpu.CompilerParams(vmem_limit_bytes=VLIM),
        cost_estimate=pl.CostEstimate(flops=0, bytes_accessed=6 << 20, transcendentals=0),
        name="line_sums",
    )(*args)


def direct(own, one, two, three, perm):
    far = lax.ppermute(two, "col", perm(2))
    low = lax.ppermute(one, "col", perm(1))
    high = lax.ppermute(three, "col", perm(-1))
    return [own, low, high, far]


def join_body(dest_ref, *refs):
    parts, outs, whole = refs[:8], refs[8 : 8 + N_SITE], refs[8 + N_SITE]
    for h in range(2):
        own, low, high, far = parts[4 * h : 4 * h + 4]
        whole[4 * h : 4 * h + 4] = own[...] + low[...] + high[...] + far[...]
    for q in range(N_SITE):
        outs[q][...] = whole[dest_ref[q]]


def join(dests, a, b):
    return pl.pallas_call(
        join_body,
        in_specs=[pl.BlockSpec(memory_space=pltpu.SMEM)] + [whole_vmem()] * 8,
        out_specs=[whole_vmem()] * N_SITE,
        out_shape=[jax.ShapeDtypeStruct((SLICE, PANEL), F32)] * N_SITE,
        scratch_shapes=[pltpu.VMEM((N_SITE, SLICE, PANEL), F32)],
        compiler_params=pltpu.CompilerParams(vmem_limit_bytes=16 << 20),
        cost_estimate=pl.CostEstimate(flops=0, bytes_accessed=5 << 19, transcendentals=0),
        name="join",
    )(dests, *a, *b)


def per_device(common_geno, rare_values, block_tile, panel_rare):
    site = lax.axis_index("site")
    col = lax.axis_index("col")
    z, core = site // 2, site % 2
    x, y = col // NY, col % NY
    order = [(dz, flip) for dz in range(NZ) for flip in range(2)]
    dests_of = {(dz, flip): (z + dz) % NZ * 2 + (core ^ flip) for dz, flip in order}
    sources_of = {(dz, flip): (z - dz) % NZ * 2 + (core ^ flip) for dz, flip in order}
    dests = jnp.stack([dests_of[one] for one in order]).astype(jnp.int32)

    tile_row = jnp.zeros((16, PANEL), BF).at[0, :BLKS].set(block_tile.astype(BF))
    panel_plus = jnp.concatenate([panel_rare, tile_row], axis=0)
    near = [panel_plus] + [
        lax.ppermute(panel_plus, "site", along_site(dz, 0)) for dz in range(1, NZ)
    ]

    scaled, panel_part = scale(common_geno)
    line = [panel_part] + [lax.ppermute(panel_part, "col", along_x(d)) for d in (1, 2, 3)]
    scaled, offsets = lax.optimization_barrier((scaled, dests * SLICE))
    received = lax.all_to_all(scaled, "col", split_axis=0, concat_axis=0, tiled=True)

    packed = pack(rare_values, offsets)
    far = [lax.ppermute(one, "site", along_site(0, 1)) for one in near]
    panels = [(near, far)[flip][dz] for dz, flip in order]
    slices = [packed[0]]
    for q in range(1, N_SITE):
        slices.append(lax.ppermute(packed[q], "site", along_site(*order[q])))

    tiles = jnp.stack([one[SBLK, :BLKS] for one in panels]).astype(jnp.int32).reshape(-1)
    tile_site, tile_col = tiles // N_COL, tiles % N_COL
    u = (tile_col // NY - x) % NX
    v = (tile_col % NY - y) % NY
    places = jnp.where(tile_site < 4, u * 16 + v * 4, HALF + v * 16 + u * 4) + tile_site % 4
    ring_parts = rare_product(places.astype(jnp.int32), slices, panels)

    line = jnp.concatenate(line, axis=0)
    plane = [line] + [lax.ppermute(line, "col", along_y(d)) for d in (1, 2, 3)]
    sites = panel_part.shape[0]
    rows = [((x - dx) % NX * NY + (y - dy) % NY) * sites for dy in range(NY) for dx in range(NX)]
    rows = jnp.stack(rows).astype(jnp.int32)

    half_dests = [dests_of[dz, flip] for flip in (1, 0) for dz in range(NZ)]
    half_dests = jnp.stack(half_dests).astype(jnp.int32)
    ring_parts, half_dests = lax.optimization_barrier((ring_parts, half_dests))
    *mine, theirs = common_product(received, half_dests, rows, plane)
    swapped = lax.ppermute(theirs, "site", along_site(0, 1))

    open_a = ring_open(*ring_parts[:2], along_x)
    open_b = ring_open(*ring_parts[5:7], along_y)
    common = [lax.ppermute(mine[dz] + swapped[dz], "site", along_site(dz, 0)) for dz in (2, 1, 3)]
    common = [mine[0], swapped] + common
    keeps = (*ring_parts[2:4], *ring_parts[7:9])
    sent = close_sums(open_a, open_b, keeps)
    closed = [
        lax.ppermute(one, "col", perm(step))
        for one, perm, step in zip(sent, (along_x, along_x, along_y, along_y), (1, -1, 1, -1))
    ]
    pre = pre_sums(open_a, open_b, ring_parts[4], ring_parts[9])
    lines = line_sums(pre, closed)
    a = direct(*lines[:4], along_y)
    b = direct(*lines[4:], along_x)
    pieces = join(dests, a, b)
    moved = {q: lax.ppermute(pieces[q], "site", along_site(*order[q])) for q in (4, 5, 2, 3, 6, 7, 1)}
    moved[0] = pieces[0]
    sources = jnp.stack([sources_of[one] * SLICE for one in order]).astype(jnp.int32)
    return finish(sources, sum_parts(common), [moved[q] for q in range(N_SITE)])


def solution(mesh):
    placed = (
        P(("site", "col"), None),
        P(("site", "col"), None, None),
        P(("site", "col")),
        P(("site", "col"), None),
    )
    return jax.shard_map(
        per_device, mesh=mesh, in_specs=placed, out_specs=P(None, ("site", "col")), check_vma=False
    )
```
